512 devices in a mesh: row: 4 (over x), col: 32 (over z_lo, y, core), depth: 4 (over z_hi).
Axes of the slice: x: 4, y: 8, z: 8 (z_hi: 4, z_lo: 2; z = z_hi * 2 + z_lo), core: 2. Of those that a mesh axis runs over, the one named last changes fastest.
Arguments:
- left_slab: bfloat16 [4096, 4096], P(None, ('col', 'depth')), may hold values from -6 to 6
- right_vectors: bfloat16 [65536, 4096], P('col', 'depth'), may hold values from -0.09375 to 0.09375
- pair_weight: float32 [4096], P(('col', 'depth')), may hold values from -6 to 6
- eigenvalue: float32 [4096], P(('col', 'depth')), may hold values from -2 to 2
- pair_order: int32 [4096], replicated, may hold values from 0 to 4095, each once
- row_offset: int32 [1], replicated, may hold values from 0 to 3072
Outputs:
- grads: bfloat16 [3, 1024, 65536], P(None, 'row', ('col', 'depth'))
The draws below stay inside these ranges and needn't reach their ends.
Inputs may be any that keep to these rules, and one draw needn't show every extreme that they name: `pair_order`: each of 0 to 4095 appears exactly once.
All inputs are finite; a program needn't handle non-finite values.
Results may differ from the reference program's by a relative error of at most 0.023.
Values may be sent and summed in bfloat16 or wider, within the bound.
No kernel may reach another device: no remote copies, remote signals or barrier semaphores. Data moves between devices by JAX's collectives and lax.ppermute only.
A program may use at most 64 MiB of HBM per device.

```python
import jax
import jax.numpy as jnp
from jax import lax

N = 65536
K = 4096
P_SIZE = 1024
SLAB = 4096
N_COL = 32
N_DEPTH = 4


def block_scale(rng, dims, shards, smallest, largest):
    gain, own = 1.0, jax.random.fold_in(rng, 6)
    for axis_at, blocks in shards:
        draws = jnp.exp(jax.random.uniform(jax.random.fold_in(own, axis_at), (blocks,), jnp.float32, smallest / len(shards), largest / len(shards)))
        gain = gain * jnp.repeat(draws, dims[axis_at] // blocks).reshape([-1 if axis == axis_at else 1 for axis in range(len(dims))])
    return gain


def centred(own_key, shape, spread, bound, shards=(), kind=jnp.bfloat16):
    loudness = block_scale(own_key, shape, shards, -0.22, 0.18) if shards else 1.0
    values = jax.random.normal(own_key, shape, jnp.float32) * spread * loudness
    return jnp.minimum(jnp.maximum(values, -bound), bound).astype(kind)


def setup_inputs(seed: int = 0) -> dict:
    arg_keys = jax.random.split(jax.random.key(seed), 7)
    left_slab = centred(arg_keys[0], (SLAB, K), 1.0, 6.0, ((1, 128),))
    right_vectors = centred(arg_keys[1], (N, K), K ** -0.5, 0.09375, ((0, 32), (1, 4)))
    pair_weight = centred(arg_keys[2], (K,), 1.0, 6.0, ((0, 128),), jnp.float32)
    eigenvalue = jnp.clip(jax.random.uniform(arg_keys[3], (K,), jnp.float32, -2.0, 2.0) * block_scale(arg_keys[3], (K,), ((0, 128),), -0.4, 0.0), -2.0, 2.0)
    pair_order = jax.random.permutation(arg_keys[4], K).astype(jnp.int32)
    row_offset = jax.random.randint(arg_keys[5], (1,), 0, SLAB - P_SIZE + 1).astype(jnp.int32)
    return dict(left_slab=left_slab, right_vectors=right_vectors, pair_weight=pair_weight, eigenvalue=eigenvalue, pair_order=pair_order, row_offset=row_offset)


def reference(left_slab, right_vectors, pair_weight, eigenvalue, pair_order, row_offset):
    panel = lax.dynamic_slice_in_dim(left_slab, row_offset[0].astype(jnp.int32), P_SIZE, 0)
    ordered = panel[:, pair_order].astype(jnp.float32)
    weight = pair_weight[pair_order]
    lam = eigenvalue[pair_order]
    powers = jnp.stack([weight, weight * lam, weight * lam * lam])
    scaled = (ordered[None, :, :] * powers[:, None, :]).astype(jnp.bfloat16).reshape(3 * P_SIZE, K)
    group_width = K // N_DEPTH
    block_cols = N // N_COL

    def column_block(index):
        start = (index * block_cols).astype(jnp.int32)
        columns = lax.dynamic_slice_in_dim(right_vectors, start, block_cols, 0)
        total = jnp.zeros((3 * P_SIZE, block_cols), jnp.float32)
        for group in range(N_DEPTH):
            lo = group * group_width
            part = lax.dot_general(scaled[:, lo:lo + group_width], columns[:, lo:lo + group_width],
                                   (((1,), (1,)), ((), ())), preferred_element_type=jnp.float32)
            total = total + part.astype(jnp.bfloat16).astype(jnp.float32)
        return total.astype(jnp.bfloat16)

    blocks = lax.map(column_block, jnp.arange(N_COL, dtype=jnp.int32))
    blocks = blocks.reshape(N_COL, 3, P_SIZE, block_cols)
    return jnp.transpose(blocks, (1, 2, 0, 3)).reshape(3, P_SIZE, N)
```

```python
import functools

import jax
import jax.numpy as jnp
from jax import lax
from jax.experimental import pallas as pl
from jax.experimental.pallas import tpu as pltpu
from jax.sharding import Mesh, PartitionSpec as P

P_SIZE = 1024
LANES = 128
TILE = 512
BLOCK = 256


def everyone(x, axes):
    n = lax.axis_size(axes)
    return lax.all_to_all(jnp.broadcast_to(x[None], (n,) + x.shape), axes, 0, 0)


def shifted(x, axis, by):
    n = lax.axis_size(axis)
    return lax.ppermute(x, axis, [(i, (i + by) % n) for i in range(n)])


def order_kernel(core_ref, order_ref, own_ref, other_ref, s_ref, lt_ref, mt_ref):
    width = 32

    @pl.when(pl.program_id(0) == 0)
    def _():
        for h, src in enumerate((own_ref, other_ref)):
            for a in range(2):
                for q in range(16):
                    blk = src[4 * q:4 * q + 4, a * width:(a + 1) * width, :].reshape(LANES, LANES)
                    lt_ref[h, a * LANES:(a + 1) * LANES, q * LANES:(q + 1) * LANES] = blk.T
            mt_ref[h] = src[:, 2 * width, :].astype(jnp.float32).T.astype(jnp.bfloat16)

    e = order_ref[...]
    j = e & 31
    q = e >> 5
    core = (q >> 2) & 1
    d = ((q >> 3) & 7) * 8 + (q >> 6) * 4 + (q & 3)
    mine = core == core_ref[0]
    storage = jnp.where(mine, d * width + j, 2048 + d * width + j)
    acc = jnp.zeros((2 * LANES, TILE), jnp.float32)
    rows = lax.broadcasted_iota(jnp.int32, (BLOCK, TILE), 0)
    for h in range(2):
        for b in range(2048 // BLOCK):
            hot = jnp.where(rows == storage - (h * 2048 + b * BLOCK), 1.0, 0.0).astype(jnp.bfloat16)
            acc += jnp.dot(lt_ref[h, :, b * BLOCK:(b + 1) * BLOCK], hot, preferred_element_type=jnp.float32)
    src_rows = lax.broadcasted_iota(jnp.int32, (64, TILE), 0)
    d_own = jnp.where(mine, d, -1)
    d_other = jnp.where(mine, -1, d)
    picked = jnp.dot(mt_ref[0], jnp.where(src_rows == d_own, 1.0, 0.0).astype(jnp.bfloat16), preferred_element_type=jnp.float32)
    picked += jnp.dot(mt_ref[1], jnp.where(src_rows == d_other, 1.0, 0.0).astype(jnp.bfloat16), preferred_element_type=jnp.float32)
    at_j = lax.broadcasted_iota(jnp.int32, (width, TILE), 0) == j
    parts = [
        jnp.sum(jnp.where(at_j, picked[i * width:(i + 1) * width], 0.0), axis=0, keepdims=True) for i in range(4)
    ]
    w = parts[0] + parts[1]
    lam = parts[2] + parts[3]
    s_ref[0, 0] = (acc * w).astype(jnp.bfloat16)
    s_ref[0, 1] = (acc * (w * lam)).astype(jnp.bfloat16)
    s_ref[0, 2] = (acc * (w * lam * lam)).astype(jnp.bfloat16)


def ordered_powers(core, pair_order, own, other):
    k = pair_order.shape[0]
    per_group = k // 4
    steps = per_group // TILE
    return pl.pallas_call(
        order_kernel,
        grid=(k // TILE,),
        in_specs=[
            pl.BlockSpec(memory_space=pltpu.SMEM),
            pl.BlockSpec((1, TILE), lambda t: (0, t)),
            pl.BlockSpec(own.shape, lambda t: (0, 0, 0)),
            pl.BlockSpec(own.shape, lambda t: (0, 0, 0)),
        ],
        out_specs=pl.BlockSpec((1, 3, 2 * LANES, TILE), lambda t: (t // steps, 0, 0, t % steps)),
        out_shape=jax.ShapeDtypeStruct((4, 3, 2 * LANES, per_group), jnp.bfloat16),
        scratch_shapes=[pltpu.VMEM((2, 2 * LANES, 2048), jnp.bfloat16), pltpu.VMEM((2, LANES, 64), jnp.bfloat16)],
        compiler_params=pltpu.CompilerParams(vmem_limit_bytes=40 * 2**20),
        cost_estimate=pl.CostEstimate(flops=2 * k * k * 256, bytes_accessed=12 * 2**20, transcendentals=0),
    )(core[None], pair_order[None], own, other)


def contract_kernel(at_ref, s_ref, own_ref, na_ref, nb_ref, a1, b1, a2, b2, a3, b3, o_ref):
    r, d = at_ref[0], at_ref[1]
    near = ((na_ref, nb_ref), (a1, b1), (a2, b2), (a3, b3))
    before, across, after = (d + 3) % 4, (d + 2) % 4, (d + 1) % 4
    nt = (((1,), (1,)), ((), ()))
    for pair in range(2):
        ts = (2 * pair, 2 * pair + 1)
        qs = [(r - t + 4) % 4 for t in ts]
        for m in range(3):
            acc = None
            for g, get in (
                (d, lambda t, q: own_ref[0, q]),
                (before, lambda t, q: near[t][0][0]),
                (after, lambda t, q: near[t][0][1]),
                (across, lambda t, q: near[t][1][...]),
            ):
                rhs = jnp.concatenate([get(t, q) for t, q in zip(ts, qs)], axis=0)
                part = lax.dot_general(s_ref[g, m], rhs, nt, preferred_element_type=jnp.float32)
                acc = part if acc is None else acc + part
            out = acc.astype(jnp.bfloat16)
            for n, q in enumerate(qs):
                o_ref[m, :, pl.ds(pl.multiple_of(q * LANES, LANES), LANES)] = out[:, n * LANES:(n + 1) * LANES]


def contract(at, s, rv, near, far):
    vm = pl.BlockSpec(memory_space=pltpu.VMEM)
    flat = [v for ab in (near, *far) for v in ab]
    grid_spec = pltpu.PrefetchScalarGridSpec(
        num_scalar_prefetch=1,
        grid=(1,),
        in_specs=[
            pl.BlockSpec(s.shape, lambda i, at: (0, 0, 0, 0)),
            pl.BlockSpec((1,) + rv.shape[1:], lambda i, at: (at[1], 0, 0, 0)),
        ] + [pl.BlockSpec(v.shape, lambda i, at, n=v.ndim: (0,) * n) for v in flat],
        out_specs=pl.BlockSpec((3, 256, 512), lambda i, at: (0, 0, 0)),
    )
    return pl.pallas_call(
        contract_kernel,
        grid_spec=grid_spec,
        out_shape=jax.ShapeDtypeStruct((3, 256, 512), jnp.bfloat16),
        compiler_params=pltpu.CompilerParams(vmem_limit_bytes=48 * 2**20),
        cost_estimate=pl.CostEstimate(flops=2 * 768 * 4096 * 512, bytes_accessed=11 * 2**20, transcendentals=0),
    )(at, s, rv, *flat)


def split(v):
    hi = lax.reduce_precision(v, 8, 7)
    return [hi.astype(jnp.bfloat16), (v - hi).astype(jnp.bfloat16)]


def on_device(left_slab, right_vectors, pair_weight, eigenvalue, pair_order, row_offset):
    n_depth, n_row = lax.axis_size("depth"), lax.axis_size("row")
    r, d = lax.axis_index("row"), lax.axis_index("depth")
    panel_rows = P_SIZE // n_row
    cols, group = right_vectors.shape
    quarter = cols // n_depth // n_row
    rv = right_vectors.reshape(n_depth, n_row, quarter, group)

    def piece(by):
        return lax.dynamic_slice(rv, ((d + by) % n_depth, r, 0, 0), (1, 1, quarter, group)).reshape(quarter, group)

    z1 = shifted(piece(1), "depth", 1)
    z3 = shifted(piece(3), "depth", 3)
    z2 = shifted(piece(2), "depth", 2)
    near = jnp.stack([z1, z3])
    far = [(shifted(near, "row", t), shifted(z2, "row", t)) for t in (1, 2, 3)]

    start = row_offset[0] + r * panel_rows
    mine = lax.dynamic_slice_in_dim(left_slab.T, start, panel_rows, 1)
    scal = jnp.concatenate(split(pair_weight) + split(eigenvalue))
    scal = jnp.broadcast_to(scal[None], (8, LANES))
    mine = jnp.concatenate([mine[:, :LANES], mine[:, LANES:], scal], axis=0)
    by_z = everyone(mine, ("zlo", "depth"))
    by_y = everyone(by_z, "y").reshape(64, 72, LANES)
    other = shifted(by_y, "core", 1)
    s = ordered_powers(lax.axis_index("core"), pair_order, by_y, other)
    return contract(jnp.stack([r, d]), s, rv, (near, z2), far)


def solution(mesh):
    fine = Mesh(mesh.devices.reshape(4, 2, 8, 2, 4), ("row", "zlo", "y", "core", "depth"))
    col = ("zlo", "y", "core")
    all_k = col + ("depth",)
    in_specs = (P(None, all_k), P(col, "depth"), P(all_k), P(all_k), P(), P())
    return jax.shard_map(on_device, mesh=fine, in_specs=in_specs, out_specs=P(None, "row", all_k), check_vma=False)
```

```python
import jax
import jax.numpy as jnp
from jax import lax
from jax.experimental import pallas as pl
from jax.experimental.pallas import tpu as pltpu
from jax.sharding import Mesh, PartitionSpec as P

P_SIZE = 1024
LANES = 128
TILE = 512
BLOCK = 256
WIDTH = 32
NT = (((1,), (1,)), ((), ()))
FREE = pl.CostEstimate(flops=1000, bytes_accessed=1000, transcendentals=0)
VM = pl.BlockSpec(memory_space=pltpu.VMEM)
SM = pl.BlockSpec(memory_space=pltpu.SMEM)
ANY = pl.BlockSpec(memory_space=pl.ANY)


def everyone(x, axes):
    n = lax.axis_size(axes)
    return lax.all_to_all(jnp.broadcast_to(x[None], (n,) + x.shape), axes, 0, 0)


def shifted(x, axis, by):
    n = lax.axis_size(axis)
    return lax.ppermute(x, axis, [(i, (i + by) % n) for i in range(n)])


def order_kernel(order_ref, src_ref, s_ref, lt_ref, mt_ref):
    width = 32

    @pl.when(pl.program_id(0) == 0)
    def _():
        for q in range(32):
            for a in range(2):
                blk = src_ref[4 * q:4 * q + 4, a * width:(a + 1) * width, :].reshape(LANES, LANES)
                lt_ref[a * LANES:(a + 1) * LANES, q * LANES:(q + 1) * LANES] = blk.T
        mt_ref[...] = src_ref[:, 2 * width, :].astype(jnp.float32).T.astype(jnp.bfloat16)

    e = order_ref[...]
    j = e & 31
    q = e >> 5
    d = ((q >> 2) & 1) * 64 + ((q >> 3) & 7) * 8 + (q >> 6) * 4 + (q & 3)
    storage = d * width + j
    acc = jnp.zeros((2 * LANES, TILE), jnp.float32)
    rows = lax.broadcasted_iota(jnp.int32, (BLOCK, TILE), 0)
    for b in range(4096 // BLOCK):
        hot = jnp.where(rows == storage - b * BLOCK, 1.0, 0.0).astype(jnp.bfloat16)
        acc += jnp.dot(lt_ref[:, b * BLOCK:(b + 1) * BLOCK], hot, preferred_element_type=jnp.float32)
    src_rows = lax.broadcasted_iota(jnp.int32, (LANES, TILE), 0)
    picked = jnp.dot(mt_ref[...], jnp.where(src_rows == d, 1.0, 0.0).astype(jnp.bfloat16), preferred_element_type=jnp.float32)
    at_j = lax.broadcasted_iota(jnp.int32, (width, TILE), 0) == j
    parts = [
        jnp.sum(jnp.where(at_j, picked[i * width:(i + 1) * width], 0.0), axis=0, keepdims=True) for i in range(4)
    ]
    w = parts[0] + parts[1]
    lam = parts[2] + parts[3]
    s_ref[0] = (acc * w).astype(jnp.bfloat16)
    s_ref[1] = (acc * (w * lam)).astype(jnp.bfloat16)
    s_ref[2] = (acc * (w * lam * lam)).astype(jnp.bfloat16)


def ordered_powers(pair_order, src):
    k = pair_order.shape[0]
    return pl.pallas_call(
        order_kernel,
        grid=(k // TILE,),
        in_specs=[
            pl.BlockSpec((1, TILE), lambda t: (0, t)),
            pl.BlockSpec(src.shape, lambda t: (0, 0, 0)),
        ],
        out_specs=pl.BlockSpec((3, 2 * LANES, TILE), lambda t: (0, 0, t)),
        out_shape=jax.ShapeDtypeStruct((3, 2 * LANES, k), jnp.bfloat16),
        scratch_shapes=[pltpu.VMEM((2 * LANES, k), jnp.bfloat16), pltpu.VMEM((LANES, LANES), jnp.bfloat16)],
        compiler_params=pltpu.CompilerParams(vmem_limit_bytes=32 * 2**20),
        cost_estimate=pl.CostEstimate(flops=2 * k * k * 256, bytes_accessed=12 * 2**20, transcendentals=0),
    )(pair_order[None], src)


def lanes(d, n, group):
    return pl.ds(pl.multiple_of(((d + n) % 4) * group, LANES), group)


def own_kernel(at_ref, s_ref, rv_ref, o_ref, rhs_ref, sem):
    d = at_ref[1]
    copy = pltpu.make_async_copy(rv_ref.at[d], rhs_ref, sem)
    copy.start()
    copy.wait()
    for m in range(3):
        for c in range(2):
            cols = slice(c * 256, (c + 1) * 256)
            o_ref[m, :, cols] = lax.dot_general(
                s_ref[m, :, lanes(d, 0, rhs_ref.shape[1])], rhs_ref[cols, :], NT, preferred_element_type=jnp.float32
            )


def contract_kernel(at_ref, s_ref, acc_ref, p0, p1, p2, p3, o_ref, rhs_ref, sum_ref, sem):
    r, d = at_ref[0], at_ref[1]
    step = p0.shape[1]
    group = rhs_ref.shape[2]
    copies = []
    for n in (1, 2, 3):
        srcs = (p0.at[(d + n) % 4], p1.at[n - 1], p2.at[(d + n) % 4], p3.at[n - 1])
        at_n = []
        for t, src in enumerate(srcs):
            rows = pl.ds(pl.multiple_of(((r - t + 4) % 4) * step, 128), step)
            at_n.append(pltpu.make_async_copy(src, rhs_ref.at[n - 1, rows], sem.at[4 * n - 4 + t]))
        copies.append(at_n)
    for at_n in copies:
        for copy in at_n:
            copy.start()
    for n in (1, 2, 3):
        for copy in copies[n - 1]:
            copy.wait()
        for c in range(2):
            cols = slice(c * 256, (c + 1) * 256)
            for m in range(3):
                acc = lax.dot_general(
                    s_ref[m, :, lanes(d, n, group)], rhs_ref[n - 1, cols, :], NT, preferred_element_type=jnp.float32
                )
                acc += acc_ref[m, :, cols] if n == 1 else sum_ref[m, :, cols]
                if n < 3:
                    sum_ref[m, :, cols] = acc
                else:
                    o_ref[m, :, cols] = acc.astype(jnp.bfloat16)


def contract(at, s, rv, parts):
    _, block, group = rv.shape
    summed = pl.pallas_call(
        own_kernel,
        in_specs=[SM, VM, ANY],
        out_specs=VM,
        out_shape=jax.ShapeDtypeStruct((3, 2 * LANES, block), jnp.float32),
        scratch_shapes=[pltpu.VMEM((block, group), jnp.bfloat16), pltpu.SemaphoreType.DMA(())],
        compiler_params=pltpu.CompilerParams(vmem_limit_bytes=24 * 2**20),
        cost_estimate=FREE,
    )(at, s, rv)
    return pl.pallas_call(
        contract_kernel,
        in_specs=[SM, VM, VM] + [ANY] * len(parts),
        out_specs=VM,
        out_shape=jax.ShapeDtypeStruct((3, 2 * LANES, block), jnp.bfloat16),
        scratch_shapes=[
            pltpu.VMEM((3, block, group), jnp.bfloat16),
            pltpu.VMEM((3, 2 * LANES, block), jnp.float32),
            pltpu.SemaphoreType.DMA((12,)),
        ],
        compiler_params=pltpu.CompilerParams(vmem_limit_bytes=24 * 2**20),
        cost_estimate=FREE,
    )(at, s, summed, *parts)


def split(v):
    hi = lax.reduce_precision(v, 8, 7)
    return [hi.astype(jnp.bfloat16), (v - hi).astype(jnp.bfloat16)]


def on_device(left_slab, right_vectors, pair_weight, eigenvalue, pair_order, row_offset):
    n_depth, n_row = lax.axis_size("depth"), lax.axis_size("row")
    r, d = lax.axis_index("row"), lax.axis_index("depth")
    at = jnp.stack([r, d])
    panel_rows = P_SIZE // n_row
    cols, group = right_vectors.shape
    block = cols // n_depth
    quarter = block // n_row

    start = row_offset[0] + r * panel_rows
    mine = lax.dynamic_slice_in_dim(left_slab.T, start, panel_rows, 1)
    scal = jnp.concatenate(split(pair_weight) + split(eigenvalue))
    scal = jnp.broadcast_to(scal[None], (8, LANES))
    mine = jnp.concatenate([mine[:, :LANES], mine[:, LANES:], scal], axis=0)
    by_z = everyone(mine, ("zlo", "depth"))
    both = lax.all_gather(by_z, ("core", "y"), axis=0, tiled=True)

    rv = right_vectors.reshape(n_depth, block, group)
    first = lax.dynamic_slice_in_dim(rv, r * quarter, quarter, 1)
    first, _ = lax.optimization_barrier((first, by_z))
    first = lax.all_to_all(first, "depth", 0, 0)
    others = jnp.concatenate([lax.dynamic_index_in_dim(first, (d + n) % n_depth, 0) for n in (1, 2, 3)])
    second = lax.dynamic_slice_in_dim(rv, ((r + 2) % n_row) * quarter, quarter, 1)
    second, _ = lax.optimization_barrier((second, others))
    second = lax.all_to_all(second, "depth", 0, 0)
    parts = [first, shifted(others, "row", 1), second, shifted(others, "row", 3)]

    both, _ = lax.optimization_barrier((both, others))
    s = ordered_powers(pair_order, both)
    return contract(at, s, rv, parts)


def solution(mesh):
    fine = Mesh(mesh.devices.reshape(4, 2, 8, 2, 4), ("row", "zlo", "y", "core", "depth"))
    col = ("zlo", "y", "core")
    all_k = col + ("depth",)
    in_specs = (P(None, all_k), P(col, "depth"), P(all_k), P(all_k), P(), P())
    return jax.shard_map(on_device, mesh=fine, in_specs=in_specs, out_specs=P(None, "row", all_k), check_vma=False)
```

```python
import jax
import jax.numpy as jnp
from jax import lax
from jax.experimental import pallas as pl
from jax.experimental.pallas import tpu as pltpu
from jax.sharding import Mesh, PartitionSpec as P

P_SIZE = 1024
LANES = 128
TILE = 1024
BLOCK = 256
WIDTH = 32
NT = (((1,), (1,)), ((), ()))
FREE = pl.CostEstimate(flops=1000, bytes_accessed=1000, transcendentals=0)
VM = pl.BlockSpec(memory_space=pltpu.VMEM)
SM = pl.BlockSpec(memory_space=pltpu.SMEM)
ANY = pl.BlockSpec(memory_space=pl.ANY)
HBM = pl.BlockSpec(memory_space=pltpu.HBM)


def everyone(x, axes):
    n = lax.axis_size(axes)
    return lax.all_to_all(jnp.broadcast_to(x[None], (n,) + x.shape), axes, 0, 0)


def shifted(x, axis, by):
    n = lax.axis_size(axis)
    return lax.ppermute(x, axis, [(i, (i + by) % n) for i in range(n)])


def order_kernel(at_ref, order_ref, own_ref, other_ref, rv_ref, s_out, acc_out, lt_ref, mt_ref, rhs_ref, s_buf, acc_ref, sem, out_sem):
    t = pl.program_id(0)
    last = pl.num_programs(0) - 1
    steps = rhs_ref.shape[1] // TILE
    copy = pltpu.make_async_copy(rv_ref.at[at_ref[1]], rhs_ref, sem)
    acc_copy = pltpu.make_async_copy(acc_ref, acc_out, out_sem.at[2])
    slot = t % 2
    s_ref = s_buf.at[slot]

    def s_copy(step, at):
        ks = pl.ds(pl.multiple_of(step * TILE, TILE), TILE)
        return pltpu.make_async_copy(s_buf.at[at], s_out.at[:, :, ks], out_sem.at[at])

    @pl.when(t == 0)
    def _():
        copy.start()
        for h, src in enumerate((own_ref, other_ref)):
            for q in range(16):
                for a in range(2):
                    blk = src[4 * q:4 * q + 4, a * WIDTH:(a + 1) * WIDTH, :].reshape(LANES, LANES)
                    at = (16 * h + q) * LANES
                    lt_ref[a * LANES:(a + 1) * LANES, at:at + LANES] = blk.T
        mt = jnp.concatenate([own_ref[:, 2 * WIDTH, :], other_ref[:, 2 * WIDTH, :]], axis=0)
        mt_ref[...] = mt.astype(jnp.float32).T.astype(jnp.bfloat16)

    e = order_ref[...]
    j = e & 31
    q = e >> 5
    d = (((q >> 2) & 1) ^ at_ref[2]) * 64 + ((q >> 3) & 7) * 8 + (q >> 6) * 4 + (q & 3)
    storage = d * WIDTH + j
    acc = jnp.zeros((2 * LANES, TILE), jnp.float32)
    rows = lax.broadcasted_iota(jnp.int32, (BLOCK, TILE), 0)
    for b in range(4096 // BLOCK):
        hot = jnp.where(rows == storage - b * BLOCK, 1.0, 0.0).astype(jnp.bfloat16)
        acc += jnp.dot(lt_ref[:, b * BLOCK:(b + 1) * BLOCK], hot, preferred_element_type=jnp.float32)
    src_rows = lax.broadcasted_iota(jnp.int32, (LANES, TILE), 0)
    hot = jnp.where(src_rows == d, 1.0, 0.0).astype(jnp.bfloat16)
    picked = jnp.dot(mt_ref[...], hot, preferred_element_type=jnp.float32)
    at_j = lax.broadcasted_iota(jnp.int32, (WIDTH, TILE), 0) == j
    parts = [jnp.sum(jnp.where(at_j, picked[i * WIDTH:(i + 1) * WIDTH], 0.0), axis=0, keepdims=True) for i in range(4)]
    w = parts[0] + parts[1]
    lam = parts[2] + parts[3]

    @pl.when(t >= 2)
    def _():
        s_copy(t - 2, slot).wait()

    s_ref[0] = (acc * w).astype(jnp.bfloat16)
    s_ref[1] = (acc * (w * lam)).astype(jnp.bfloat16)
    s_ref[2] = (acc * (w * lam * lam)).astype(jnp.bfloat16)

    s_copy(t, slot).start()

    @pl.when(t == at_ref[1] * steps)
    def _():
        copy.wait()
        acc_ref[...] = jnp.zeros_like(acc_ref)

    @pl.when(t // steps == at_ref[1])
    def _():
        ks = pl.ds(pl.multiple_of((t % steps) * TILE, TILE), TILE)
        for m in range(3):
            for c in range(2):
                cols = slice(c * 256, (c + 1) * 256)
                acc_ref[m, :, cols] += lax.dot_general(
                    s_ref[m], rhs_ref[cols, ks], NT, preferred_element_type=jnp.float32
                )

    @pl.when(t == (at_ref[1] + 1) * steps - 1)
    def _():
        acc_copy.start()

    @pl.when(t == last)
    def _():
        s_copy(t - 1, 1 - slot).wait()
        s_copy(t, slot).wait()
        acc_copy.wait()


def ordered_powers(at, pair_order, own, other, rv):
    k = pair_order.shape[0]
    _, block, group = rv.shape
    whole = pl.BlockSpec(own.shape, lambda t: (0, 0, 0))
    return pl.pallas_call(
        order_kernel,
        grid=(k // TILE,),
        in_specs=[SM, pl.BlockSpec((1, TILE), lambda t: (0, t)), whole, whole, ANY],
        out_specs=[HBM, HBM],
        out_shape=[
            pltpu.HBM((3, 2 * LANES, k), jnp.bfloat16),
            pltpu.HBM((3, 2 * LANES, block), jnp.float32),
        ],
        scratch_shapes=[
            pltpu.VMEM((2 * LANES, k), jnp.bfloat16),
            pltpu.VMEM((LANES, LANES), jnp.bfloat16),
            pltpu.VMEM((block, group), jnp.bfloat16),
            pltpu.VMEM((2, 3, 2 * LANES, TILE), jnp.bfloat16),
            pltpu.VMEM((3, 2 * LANES, block), jnp.float32),
            pltpu.SemaphoreType.DMA(()),
            pltpu.SemaphoreType.DMA((3,)),
        ],
        compiler_params=pltpu.CompilerParams(vmem_limit_bytes=24 * 2**20),
        cost_estimate=FREE,
    )(at, pair_order[None], own, other, pltpu.with_memory_space_constraint(rv, pltpu.HBM))


def lanes(d, n, group):
    return pl.ds(pl.multiple_of(((d + n) % 4) * group, LANES), group)


def contract_kernel(at_ref, s_ref, acc_ref, p0, p1, p2, p3, o_ref, rhs_ref, sum_ref, s_buf, sem):
    r, d = at_ref[0], at_ref[1]
    step = p0.shape[1]
    group = rhs_ref.shape[2]
    copies = []
    for n in (1, 2, 3):
        at_n = [pltpu.make_async_copy(s_ref.at[:, :, lanes(d, n, group)], s_buf.at[n - 1], sem.at[5 * n - 5])]
        for t, src in enumerate((p0.at[n - 1], p1.at[n - 1], p2.at[(d + n) % 4], p3.at[n - 1])):
            rows = pl.ds(pl.multiple_of(((r - t + 4) % 4) * step, LANES), step)
            at_n.append(pltpu.make_async_copy(src, rhs_ref.at[n - 1, rows], sem.at[5 * n - 4 + t]))
        copies.append(at_n)
    copies[0].append(pltpu.make_async_copy(acc_ref, sum_ref, sem.at[15]))
    for at_n in copies:
        for copy in at_n:
            copy.start()
    for n in (1, 2, 3):
        for copy in copies[n - 1]:
            copy.wait()
        for c in range(2):
            cols = slice(c * 256, (c + 1) * 256)
            for m in range(3):
                acc = sum_ref[m, :, cols] + lax.dot_general(
                    s_buf[n - 1, m], rhs_ref[n - 1, cols, :], NT, preferred_element_type=jnp.float32
                )
                if n < 3:
                    sum_ref[m, :, cols] = acc
                else:
                    o_ref[m, :, cols] = acc.astype(jnp.bfloat16)


def contract(at, s, summed, parts):
    group, block = parts[0].shape[2], 4 * parts[0].shape[1]
    return pl.pallas_call(
        contract_kernel,
        in_specs=[SM, HBM, HBM] + [ANY] * len(parts),
        out_specs=VM,
        out_shape=jax.ShapeDtypeStruct((3, 2 * LANES, block), jnp.bfloat16),
        scratch_shapes=[
            pltpu.VMEM((3, block, group), jnp.bfloat16),
            pltpu.VMEM((3, 2 * LANES, block), jnp.float32),
            pltpu.VMEM((3, 3, 2 * LANES, group), jnp.bfloat16),
            pltpu.SemaphoreType.DMA((16,)),
        ],
        compiler_params=pltpu.CompilerParams(vmem_limit_bytes=20 * 2**20),
        cost_estimate=FREE,
    )(at, *(pltpu.with_memory_space_constraint(v, pltpu.HBM) for v in (s, summed)), *parts)


def split(v):
    hi = lax.reduce_precision(v, 8, 7)
    return [hi.astype(jnp.bfloat16), (v - hi).astype(jnp.bfloat16)]


def on_device(left_slab, right_vectors, pair_weight, eigenvalue, pair_order, row_offset):
    n_depth, n_row = lax.axis_size("depth"), lax.axis_size("row")
    r, d = lax.axis_index("row"), lax.axis_index("depth")
    at = jnp.stack([r, d, lax.axis_index("core")])
    panel_rows = P_SIZE // n_row
    cols, group = right_vectors.shape
    block = cols // n_depth
    quarter = block // n_row

    start = row_offset[0] + r * panel_rows
    mine = lax.dynamic_slice_in_dim(left_slab.T, start, panel_rows, 1)
    scal = jnp.concatenate(split(pair_weight) + split(eigenvalue))
    scal = jnp.broadcast_to(scal[None], (8, LANES))
    mine = jnp.concatenate([mine[:, :LANES], mine[:, LANES:], scal], axis=0)
    by_z = everyone(mine, ("zlo", "depth"))
    same = everyone(by_z, "y").reshape(64, 72, LANES)

    rv = right_vectors.reshape(n_depth, block, group)

    def first(n):
        piece = lax.dynamic_slice(rv, ((d - n) % n_depth, r * quarter, 0), (1, quarter, group))
        return shifted(piece, "depth", n_depth - n)

    others = jnp.concatenate([first(n) for n in (1, 2, 3)])
    same, others = lax.optimization_barrier((same, others))
    rv_later, _ = lax.optimization_barrier((rv, by_z))
    second = lax.dynamic_slice_in_dim(rv_later, ((r + 2) % n_row) * quarter, quarter, 1)
    second, _ = lax.optimization_barrier((second, others))
    second = lax.all_to_all(second, "depth", 0, 0)
    parts = [others, shifted(others, "row", 1), second, shifted(others, "row", 3)]

    other = shifted(same, "core", 1)
    s, summed = ordered_powers(at, pair_order, same, other, rv)
    return contract(at, s, summed, parts)


def solution(mesh):
    fine = Mesh(mesh.devices.reshape(4, 2, 8, 2, 4), ("row", "zlo", "y", "core", "depth"))
    col = ("zlo", "y", "core")
    all_k = col + ("depth",)
    in_specs = (P(None, all_k), P(col, "depth"), P(all_k), P(all_k), P(), P())
    return jax.shard_map(on_device, mesh=fine, in_specs=in_specs, out_specs=P(None, "row", all_k), check_vma=False)
```

```python
import jax
import jax.numpy as jnp
from jax import lax
from jax.experimental import pallas as pl
from jax.experimental.pallas import tpu as pltpu
from jax.sharding import Mesh, PartitionSpec as P

P_SIZE = 1024
LANES = 128
TILE = 1024
BLOCK = 256
WIDTH = 32
NT = (((1,), (1,)), ((), ()))
FREE = pl.CostEstimate(flops=1000, bytes_accessed=1000, transcendentals=0)
VM = pl.BlockSpec(memory_space=pltpu.VMEM)
SM = pl.BlockSpec(memory_space=pltpu.SMEM)
ANY = pl.BlockSpec(memory_space=pl.ANY)
HBM = pl.BlockSpec(memory_space=pltpu.HBM)


def everyone(x, axes):
    n = lax.axis_size(axes)
    return lax.all_to_all(jnp.broadcast_to(x[None], (n,) + x.shape), axes, 0, 0)


def shifted(x, axis, by):
    n = lax.axis_size(axis)
    return lax.ppermute(x, axis, [(i, (i + by) % n) for i in range(n)])


def order_kernel(at_ref, order_ref, own_ref, other_ref, rv_ref, s_out, acc_out, lt_ref, mt_ref, rhs_ref, s_buf, acc_ref, acc_buf, sem, out_sem):
    t = pl.program_id(0)
    last = pl.num_programs(0) - 1
    steps = rhs_ref.shape[1] // TILE
    copy = pltpu.make_async_copy(rv_ref.at[at_ref[1]], rhs_ref, sem)
    acc_copy = pltpu.make_async_copy(acc_buf, acc_out, out_sem.at[2])
    slot = t % 2
    s_ref = s_buf.at[slot]

    def s_copy(step, at):
        ks = pl.ds(pl.multiple_of(step * TILE, TILE), TILE)
        return pltpu.make_async_copy(s_buf.at[at], s_out.at[:, :, ks], out_sem.at[at])

    @pl.when(t == 0)
    def _():
        copy.start()
        for h, src in enumerate((own_ref, other_ref)):
            for q in range(16):
                for a in range(2):
                    blk = src[4 * q:4 * q + 4, a * WIDTH:(a + 1) * WIDTH, :].reshape(LANES, LANES)
                    at = (16 * h + q) * LANES
                    lt_ref[a * LANES:(a + 1) * LANES, at:at + LANES] = blk.T
        mt = jnp.concatenate([own_ref[:, 2 * WIDTH, :], other_ref[:, 2 * WIDTH, :]], axis=0)
        mt_ref[...] = mt.astype(jnp.float32).T.astype(jnp.bfloat16)

    e = order_ref[...]
    j = e & 31
    q = e >> 5
    d = (((q >> 2) & 1) ^ at_ref[2]) * 64 + ((q >> 3) & 7) * 8 + (q >> 6) * 4 + (q & 3)
    storage = d * WIDTH + j
    acc = jnp.zeros((2 * LANES, TILE), jnp.float32)
    rows = lax.broadcasted_iota(jnp.int32, (BLOCK, TILE), 0)
    for b in range(4096 // BLOCK):
        hot = jnp.where(rows == storage - b * BLOCK, 1.0, 0.0).astype(jnp.bfloat16)
        acc += jnp.dot(lt_ref[:, b * BLOCK:(b + 1) * BLOCK], hot, preferred_element_type=jnp.float32)
    src_rows = lax.broadcasted_iota(jnp.int32, (LANES, TILE), 0)
    hot = jnp.where(src_rows == d, 1.0, 0.0).astype(jnp.bfloat16)
    picked = jnp.dot(mt_ref[...], hot, preferred_element_type=jnp.float32)
    at_j = lax.broadcasted_iota(jnp.int32, (WIDTH, TILE), 0) == j
    parts = [jnp.sum(jnp.where(at_j, picked[i * WIDTH:(i + 1) * WIDTH], 0.0), axis=0, keepdims=True) for i in range(4)]
    w = parts[0] + parts[1]
    lam = parts[2] + parts[3]

    @pl.when(t >= 2)
    def _():
        s_copy(t - 2, slot).wait()

    s_ref[0] = (acc * w).astype(jnp.bfloat16)
    s_ref[1] = (acc * (w * lam)).astype(jnp.bfloat16)
    s_ref[2] = (acc * (w * lam * lam)).astype(jnp.bfloat16)

    s_copy(t, slot).start()

    @pl.when(t == at_ref[1] * steps)
    def _():
        copy.wait()
        acc_ref[...] = jnp.zeros_like(acc_ref)

    @pl.when(t // steps == at_ref[1])
    def _():
        ks = pl.ds(pl.multiple_of((t % steps) * TILE, TILE), TILE)
        for m in range(3):
            for c in range(2):
                cols = slice(c * 256, (c + 1) * 256)
                acc_ref[m, :, cols] += lax.dot_general(
                    s_ref[m], rhs_ref[cols, ks], NT, preferred_element_type=jnp.float32
                )

    @pl.when(t == (at_ref[1] + 1) * steps - 1)
    def _():
        acc_buf[...] = acc_ref[...].astype(jnp.bfloat16)
        acc_copy.start()

    @pl.when(t == last)
    def _():
        s_copy(t - 1, 1 - slot).wait()
        s_copy(t, slot).wait()
        acc_copy.wait()


def ordered_powers(at, pair_order, own, other, rv):
    k = pair_order.shape[0]
    _, block, group = rv.shape
    whole = pl.BlockSpec(own.shape, lambda t: (0, 0, 0))
    return pl.pallas_call(
        order_kernel,
        grid=(k // TILE,),
        in_specs=[SM, pl.BlockSpec((1, TILE), lambda t: (0, t)), whole, whole, ANY],
        out_specs=[HBM, HBM],
        out_shape=[
            pltpu.HBM((3, 2 * LANES, k), jnp.bfloat16),
            pltpu.HBM((3, 2 * LANES, block), jnp.bfloat16),
        ],
        scratch_shapes=[
            pltpu.VMEM((2 * LANES, k), jnp.bfloat16),
            pltpu.VMEM((LANES, LANES), jnp.bfloat16),
            pltpu.VMEM((block, group), jnp.bfloat16),
            pltpu.VMEM((2, 3, 2 * LANES, TILE), jnp.bfloat16),
            pltpu.VMEM((3, 2 * LANES, block), jnp.float32),
            pltpu.VMEM((3, 2 * LANES, block), jnp.bfloat16),
            pltpu.SemaphoreType.DMA(()),
            pltpu.SemaphoreType.DMA((3,)),
        ],
        compiler_params=pltpu.CompilerParams(vmem_limit_bytes=24 * 2**20),
        cost_estimate=FREE,
    )(at, pair_order[None], own, other, pltpu.with_memory_space_constraint(rv, pltpu.HBM))


def lanes(d, n, group):
    return pl.ds(pl.multiple_of(((d + n) % 4) * group, LANES), group)


def contract_kernel(at_ref, s_ref, own_ref, p0, p1, p2, p3, out_ref, rhs_ref, sum_ref, own_buf, s_buf, o_buf, sem, out_sem):
    r, d = at_ref[0], at_ref[1]
    step = p0.shape[1]
    group = rhs_ref.shape[2]
    half = 2 * step
    copies = []
    for n in (1, 2, 3):
        at_n = []
        for t, src in enumerate((p0.at[n - 1], p1.at[n - 1], p2.at[(d + n) % 4], p3.at[n - 1])):
            rows = pl.ds(pl.multiple_of(((r - t + 4) % 4) * step, LANES), step)
            at_n.append(pltpu.make_async_copy(src, rhs_ref.at[n - 1, rows], sem.at[5 * n - 5 + t]))
        at_n.append(pltpu.make_async_copy(s_ref.at[:, :, lanes(d, n, group)], s_buf.at[n - 1], sem.at[5 * n - 1]))
        copies.append(at_n)
    copies[2].append(pltpu.make_async_copy(own_ref, own_buf, sem.at[15]))
    for at_n in copies:
        for copy in at_n:
            copy.start()
    outs = []
    for n in (1, 2, 3):
        for copy in copies[n - 1]:
            copy.wait()
        for c in range(2):
            cols = slice(c * half, (c + 1) * half)
            for m in range(3):
                acc = lax.dot_general(s_buf[n - 1, m], rhs_ref[n - 1, cols, :], NT, preferred_element_type=jnp.float32)
                if n > 1:
                    acc += sum_ref[m, :, cols]
                if n < 3:
                    sum_ref[m, :, cols] = acc
                else:
                    o_buf[m, :, cols] = (acc + own_buf[m, :, cols].astype(jnp.float32)).astype(jnp.bfloat16)
            if n == 3:
                outs.append(pltpu.make_async_copy(o_buf.at[:, :, cols], out_ref.at[:, :, cols], out_sem.at[c]))
                outs[-1].start()
    for copy in outs:
        copy.wait()


def contract(at, s, summed, parts):
    group, block = parts[0].shape[2], 4 * parts[0].shape[1]
    shape = (3, 2 * LANES, block)
    return pl.pallas_call(
        contract_kernel,
        in_specs=[SM, HBM, HBM] + [ANY] * len(parts),
        out_specs=ANY,
        out_shape=jax.ShapeDtypeStruct(shape, jnp.bfloat16),
        scratch_shapes=[
            pltpu.VMEM((3, block, group), jnp.bfloat16),
            pltpu.VMEM(shape, jnp.float32),
            pltpu.VMEM(shape, jnp.bfloat16),
            pltpu.VMEM((3, 3, 2 * LANES, group), jnp.bfloat16),
            pltpu.VMEM(shape, jnp.bfloat16),
            pltpu.SemaphoreType.DMA((16,)),
            pltpu.SemaphoreType.DMA((2,)),
        ],
        compiler_params=pltpu.CompilerParams(vmem_limit_bytes=20 * 2**20),
        cost_estimate=FREE,
    )(at, *(pltpu.with_memory_space_constraint(v, pltpu.HBM) for v in (s, summed)), *parts)


def split(v):
    hi = lax.reduce_precision(v, 8, 7)
    return [hi.astype(jnp.bfloat16), (v - hi).astype(jnp.bfloat16)]


def on_device(left_slab, right_vectors, pair_weight, eigenvalue, pair_order, row_offset):
    n_depth, n_row = lax.axis_size("depth"), lax.axis_size("row")
    r, d = lax.axis_index("row"), lax.axis_index("depth")
    at = jnp.stack([r, d, lax.axis_index("core")])
    panel_rows = P_SIZE // n_row
    cols, group = right_vectors.shape
    block = cols // n_depth
    quarter = block // n_row

    start = row_offset[0] + r * panel_rows
    mine = lax.dynamic_slice_in_dim(left_slab.T, start, panel_rows, 1)
    scal = jnp.concatenate(split(pair_weight) + split(eigenvalue))
    scal = jnp.broadcast_to(scal[None], (8, LANES))
    mine = jnp.concatenate([mine[:, :LANES], mine[:, LANES:], scal], axis=0)
    by_z = everyone(mine, ("zlo", "depth"))
    same = everyone(by_z, "y").reshape(64, 72, LANES)

    rv = right_vectors.reshape(n_depth, block, group)

    def first(n):
        piece = lax.dynamic_slice(rv, ((d - n) % n_depth, r * quarter, 0), (1, quarter, group))
        return shifted(piece, "depth", n_depth - n)

    others = jnp.concatenate([first(n) for n in (1, 2, 3)])
    same, others = lax.optimization_barrier((same, others))
    rv_later, _ = lax.optimization_barrier((rv, by_z))
    second = lax.dynamic_slice_in_dim(rv_later, ((r + 2) % n_row) * quarter, quarter, 1)
    second, _ = lax.optimization_barrier((second, others))
    second = lax.all_to_all(second, "depth", 0, 0)
    parts = [others, shifted(others, "row", 1), second, shifted(others, "row", 3)]

    other = shifted(same, "core", 1)
    s, summed = ordered_powers(at, pair_order, same, other, rv)
    return contract(at, s, summed, parts)


def solution(mesh):
    fine = Mesh(mesh.devices.reshape(4, 2, 8, 2, 4), ("row", "zlo", "y", "core", "depth"))
    col = ("zlo", "y", "core")
    all_k = col + ("depth",)
    in_specs = (P(None, all_k), P(col, "depth"), P(all_k), P(all_k), P(), P())
    return jax.shard_map(on_device, mesh=fine, in_specs=in_specs, out_specs=P(None, "row", all_k), check_vma=False)
```

```python
import jax
import jax.numpy as jnp
from jax import lax
from jax.experimental import pallas as pl
from jax.experimental.pallas import tpu as pltpu
from jax.sharding import Mesh, PartitionSpec as P

P_SIZE = 1024
LANES = 128
TILE = 1024
BLOCK = 256
WIDTH = 32
NT = (((1,), (1,)), ((), ()))
FREE = pl.CostEstimate(flops=1000, bytes_accessed=1000, transcendentals=0)
VM = pl.BlockSpec(memory_space=pltpu.VMEM)
SM = pl.BlockSpec(memory_space=pltpu.SMEM)
ANY = pl.BlockSpec(memory_space=pl.ANY)
HBM = pl.BlockSpec(memory_space=pltpu.HBM)


def everyone(x, axes):
    n = lax.axis_size(axes)
    return lax.all_to_all(jnp.broadcast_to(x[None], (n,) + x.shape), axes, 0, 0)


def shifted(x, axis, by):
    n = lax.axis_size(axis)
    return lax.ppermute(x, axis, [(i, (i + by) % n) for i in range(n)])


def order_kernel(at_ref, order_ref, own_ref, other_ref, rv_ref, s_out, acc_out, lt_ref, mt_ref, rhs_ref, s_buf, acc_ref, acc_buf, sem, out_sem):
    t = pl.program_id(0)
    last = pl.num_programs(0) - 1
    steps = rhs_ref.shape[1] // TILE
    copy = pltpu.make_async_copy(rv_ref.at[at_ref[1]], rhs_ref, sem)
    acc_copy = pltpu.make_async_copy(acc_buf, acc_out, out_sem.at[2])
    slot = t % 2
    s_ref = s_buf.at[slot]

    def s_copy(step, at):
        ks = pl.ds(pl.multiple_of(step * TILE, TILE), TILE)
        return pltpu.make_async_copy(s_buf.at[at], s_out.at[:, :, ks], out_sem.at[at])

    @pl.when(t == 0)
    def _():
        copy.start()
        for h, src in enumerate((own_ref, other_ref)):
            for q in range(16):
                for a in range(2):
                    rows = src[q // 2, (q % 2) * 256:(q % 2 + 1) * 256, :].reshape(4, 2 * WIDTH, LANES)
                    blk = rows[:, a * WIDTH:(a + 1) * WIDTH, :].reshape(LANES, LANES)
                    at = (16 * h + q) * LANES
                    lt_ref[a * LANES:(a + 1) * LANES, at:at + LANES] = blk.T
        mt = jnp.concatenate([ref[:, 512:, :].astype(jnp.float32).reshape(64, LANES) for ref in (own_ref, other_ref)], axis=0)
        mt_ref[...] = mt.T.astype(jnp.bfloat16)

    e = order_ref[...]
    j = e & 31
    q = e >> 5
    d = (((q >> 2) & 1) ^ at_ref[2]) * 64 + ((q >> 3) & 7) * 8 + (q >> 6) * 4 + (q & 3)
    storage = d * WIDTH + j
    acc = jnp.zeros((2 * LANES, TILE), jnp.float32)
    rows = lax.broadcasted_iota(jnp.int32, (BLOCK, TILE), 0)
    for b in range(4096 // BLOCK):
        hot = jnp.where(rows == storage - b * BLOCK, 1.0, 0.0).astype(jnp.bfloat16)
        acc += jnp.dot(lt_ref[:, b * BLOCK:(b + 1) * BLOCK], hot, preferred_element_type=jnp.float32)
    src_rows = lax.broadcasted_iota(jnp.int32, (LANES, TILE), 0)
    hot = jnp.where(src_rows == d, 1.0, 0.0).astype(jnp.bfloat16)
    picked = jnp.dot(mt_ref[...], hot, preferred_element_type=jnp.float32)
    at_j = lax.broadcasted_iota(jnp.int32, (WIDTH, TILE), 0) == j
    parts = [jnp.sum(jnp.where(at_j, picked[i * WIDTH:(i + 1) * WIDTH], 0.0), axis=0, keepdims=True) for i in range(4)]
    w = parts[0] + parts[1]
    lam = parts[2] + parts[3]

    @pl.when(t >= 2)
    def _():
        s_copy(t - 2, slot).wait()

    s_ref[0] = (acc * w).astype(jnp.bfloat16)
    s_ref[1] = (acc * (w * lam)).astype(jnp.bfloat16)
    s_ref[2] = (acc * (w * lam * lam)).astype(jnp.bfloat16)

    s_copy(t, slot).start()

    @pl.when(t == at_ref[1] * steps)
    def _():
        copy.wait()
        acc_ref[...] = jnp.zeros_like(acc_ref)

    @pl.when(t // steps == at_ref[1])
    def _():
        ks = pl.ds(pl.multiple_of((t % steps) * TILE, TILE), TILE)
        for m in range(3):
            for c in range(2):
                cols = slice(c * 256, (c + 1) * 256)
                acc_ref[m, :, cols] += lax.dot_general(
                    s_ref[m], rhs_ref[cols, ks], NT, preferred_element_type=jnp.float32
                )

    @pl.when(t == (at_ref[1] + 1) * steps - 1)
    def _():
        acc_buf[...] = acc_ref[...].astype(jnp.bfloat16)
        acc_copy.start()

    @pl.when(t == last)
    def _():
        s_copy(t - 1, 1 - slot).wait()
        s_copy(t, slot).wait()
        acc_copy.wait()


def ordered_powers(at, pair_order, own, other, rv):
    k = pair_order.shape[0]
    _, block, group = rv.shape
    whole = pl.BlockSpec(own.shape, lambda t: (0, 0, 0))
    return pl.pallas_call(
        order_kernel,
        grid=(k // TILE,),
        in_specs=[SM, pl.BlockSpec((1, TILE), lambda t: (0, t)), whole, whole, ANY],
        out_specs=[HBM, HBM],
        out_shape=[
            pltpu.HBM((3, 2 * LANES, k), jnp.bfloat16),
            pltpu.HBM((3, 2 * LANES, block), jnp.bfloat16),
        ],
        scratch_shapes=[
            pltpu.VMEM((2 * LANES, k), jnp.bfloat16),
            pltpu.VMEM((LANES, LANES), jnp.bfloat16),
            pltpu.VMEM((block, group), jnp.bfloat16),
            pltpu.VMEM((2, 3, 2 * LANES, TILE), jnp.bfloat16),
            pltpu.VMEM((3, 2 * LANES, block), jnp.float32),
            pltpu.VMEM((3, 2 * LANES, block), jnp.bfloat16),
            pltpu.SemaphoreType.DMA(()),
            pltpu.SemaphoreType.DMA((3,)),
        ],
        compiler_params=pltpu.CompilerParams(vmem_limit_bytes=24 * 2**20),
        cost_estimate=FREE,
    )(at, pair_order[None], own, other, pltpu.with_memory_space_constraint(rv, pltpu.HBM))


def lanes(d, n, group):
    return pl.ds(pl.multiple_of(((d + n) % 4) * group, LANES), group)


def contract_kernel(at_ref, s_ref, own_ref, p0, p1, p2, p3, out_ref, rhs_ref, sum_ref, own_buf, s_buf, o_buf, sem, out_sem):
    r, d = at_ref[0], at_ref[1]
    step, group = p0.shape[1], p0.shape[2]
    half = 2 * step
    quarters = ((r, (r + 2) % 4), ((r + 3) % 4, (r + 1) % 4))
    copies = []
    for n in (1, 2, 3):
        copies.append(pltpu.make_async_copy(s_ref.at[:, :, lanes(d, n, group)], s_buf.at[n - 1], sem.at[3 * n - 3]))
        copies.append(pltpu.make_async_copy(p1.at[n - 1], rhs_ref.at[n - 1, :step], sem.at[3 * n - 2]))
        copies.append(pltpu.make_async_copy(p3.at[n - 1], rhs_ref.at[n - 1, step:], sem.at[3 * n - 1]))
    copies.append(pltpu.make_async_copy(own_ref, own_buf, sem.at[9]))
    for copy in copies:
        copy.start()
    outs = []
    for n in (1, 2, 3):
        for copy in copies[3 * n - 3:3 * n]:
            copy.wait()
        if n == 3:
            copies[9].wait()
        rhs = (jnp.concatenate([p0[n - 1], p2[(d + n) % 4]], axis=0), rhs_ref[n - 1])
        for m in range(3):
            for c in range(2):
                cols = slice(c * half, (c + 1) * half)
                acc = lax.dot_general(s_buf[n - 1, m], rhs[c], NT, preferred_element_type=jnp.float32)
                if n > 1:
                    acc += sum_ref[m, :, cols]
                if n < 3:
                    sum_ref[m, :, cols] = acc
                    continue
                for a, q in enumerate(quarters[c]):
                    at = pl.ds(pl.multiple_of(q * step, LANES), step)
                    own = own_buf[m, :, at].astype(jnp.float32)
                    o_buf[m, :, at] = (acc[:, a * step:(a + 1) * step] + own).astype(jnp.bfloat16)
            if n == 3:
                outs.append(pltpu.make_async_copy(o_buf.at[m], out_ref.at[m], out_sem.at[m]))
                outs[-1].start()
    for copy in outs:
        copy.wait()


def contract(at, s, summed, parts):
    step, group = parts[0].shape[1], parts[0].shape[2]
    shape = (3, 2 * LANES, 4 * step)
    return pl.pallas_call(
        contract_kernel,
        in_specs=[SM, HBM, HBM, VM, ANY, VM, ANY],
        out_specs=ANY,
        out_shape=jax.ShapeDtypeStruct(shape, jnp.bfloat16),
        scratch_shapes=[
            pltpu.VMEM((3, 2 * step, group), jnp.bfloat16),
            pltpu.VMEM(shape, jnp.float32),
            pltpu.VMEM(shape, jnp.bfloat16),
            pltpu.VMEM((3, 3, 2 * LANES, group), jnp.bfloat16),
            pltpu.VMEM(shape, jnp.bfloat16),
            pltpu.SemaphoreType.DMA((10,)),
            pltpu.SemaphoreType.DMA((3,)),
        ],
        compiler_params=pltpu.CompilerParams(vmem_limit_bytes=20 * 2**20),
        cost_estimate=FREE,
    )(at, *(pltpu.with_memory_space_constraint(v, pltpu.HBM) for v in (s, summed)), *parts)


def split(v):
    hi = lax.reduce_precision(v, 8, 7)
    return [hi.astype(jnp.bfloat16), (v - hi).astype(jnp.bfloat16)]


def on_device(left_slab, right_vectors, pair_weight, eigenvalue, pair_order, row_offset):
    n_depth, n_row = lax.axis_size("depth"), lax.axis_size("row")
    r, d = lax.axis_index("row"), lax.axis_index("depth")
    at = jnp.stack([r, d, lax.axis_index("core")])
    panel_rows = P_SIZE // n_row
    cols, group = right_vectors.shape
    block = cols // n_depth
    quarter = block // n_row

    start = row_offset[0] + r * panel_rows
    mine = lax.dynamic_slice_in_dim(left_slab.T, start, panel_rows, 1)
    scal = jnp.concatenate(split(pair_weight) + split(eigenvalue))
    scal = jnp.broadcast_to(scal[None], (8, LANES))
    mine = jnp.concatenate([mine[:, :LANES], mine[:, LANES:], scal], axis=0)
    by_z = everyone(mine, ("zlo", "depth"))
    by_z = jnp.concatenate([by_z[:, :2 * WIDTH].reshape(-1, LANES), by_z[:, 2 * WIDTH]])
    same = everyone(by_z, "y")

    rv = right_vectors.reshape(n_depth, block, group)

    def first(n):
        piece = lax.dynamic_slice(rv, ((d - n) % n_depth, r * quarter, 0), (1, quarter, group))
        return shifted(piece, "depth", n_depth - n)

    others = jnp.concatenate([first(n) for n in (1, 2, 3)])
    same, others = lax.optimization_barrier((same, others))
    rv_later, _ = lax.optimization_barrier((rv, by_z))
    second = lax.dynamic_slice_in_dim(rv_later, ((r + 2) % n_row) * quarter, quarter, 1)
    second, _ = lax.optimization_barrier((second, others))
    second = lax.all_to_all(second, "depth", 0, 0)
    parts = [others, shifted(others, "row", 1), second, shifted(others, "row", 3)]

    other = shifted(same, "core", 1)
    s, summed = ordered_powers(at, pair_order, same, other, rv)
    return contract(at, s, summed, parts)


def solution(mesh):
    fine = Mesh(mesh.devices.reshape(4, 2, 8, 2, 4), ("row", "zlo", "y", "core", "depth"))
    col = ("zlo", "y", "core")
    all_k = col + ("depth",)
    in_specs = (P(None, all_k), P(col, "depth"), P(all_k), P(all_k), P(), P())
    return jax.shard_map(on_device, mesh=fine, in_specs=in_specs, out_specs=P(None, "row", all_k), check_vma=False)
```
